1024 devices in a mesh: seq: 32 (over y_hi, z), res: 32 (over y_lo, x, core).
Axes of the slice: x: 8, y: 8 (y_hi: 4, y_lo: 2; y = y_hi * 2 + y_lo), z: 8, core: 2. Of those that a mesh axis runs over, the one named last changes fastest.
Arguments:
- incoming_homolog_features: bfloat16 [512, 1024, 256], P('seq', 'res'), may hold values from -6 to 6
- alignment_token_index: int32 [512, 1024], P('seq', 'res'), may hold values from 0 to 22
- sequence_mask: int32 [512], replicated, may hold values 0 or 1
- symbol_vector_lookup: bfloat16 [23, 256], replicated, may hold values from -6 to 6
- query_weight: bfloat16 [256, 256], replicated, may hold values from -12 to 12
- lookup_label_matrix: bfloat16 [256, 256], replicated, may hold values from -0.375 to 0.375
- content_matrix: bfloat16 [256, 256], replicated, may hold values from -0.375 to 0.375
- sigmoid_switch_matrix: bfloat16 [256, 256], replicated, may hold values from -0.375 to 0.375
- final_mixing_matrix: bfloat16 [256, 256], replicated, may hold values from -0.375 to 0.375
- first_operand_matrix: bfloat16 [256, 32], replicated, may hold values from -0.375 to 0.375
- second_operand_matrix: bfloat16 [256, 32], replicated, may hold values from -0.375 to 0.375
- pair_weight: bfloat16 [1024, 128], replicated, may hold values from -4 to 4
Outputs:
- revised_homolog_features: bfloat16 [512, 1024, 256], P('seq', 'res')
- pair_output: float32 [1024, 32, 32, 128], P('res', 'seq')
The draws below stay inside these ranges and needn't reach their ends.
All inputs are finite; a program needn't handle non-finite values.
Results may differ from the reference program's by a relative error of at most 0.012.
The reference program's roundings to bfloat16 on the way count: a program that leaves them out, or rounds other values in their place, can miss the bound.
Values may be sent and summed in bfloat16 or wider, within the bound.
A program may use at most 64 MiB of HBM per device.

```python
import math
import jax
import jax.numpy as jnp
import numpy as np
from jax import lax

FEATURE_DEPTH = 256
HEAD_NUMBER = 8
SUBSPACE_SIZE = 32
PRODUCT_DEPTH = 32
CZ = 128
SYMBOL_KINDS = 23
RES_DEV = 32
HOMOLOG_TOTAL = 512
CHAIN_LENGTH = 1024
N_RES = 32


def draw_query_weight(key, part):
    random_seed_source = jax.random.fold_in(jax.random.fold_in(key, 7), 0)
    content_vectors = jax.random.normal(random_seed_source, (FEATURE_DEPTH, HEAD_NUMBER * SUBSPACE_SIZE), jnp.float32) * FEATURE_DEPTH ** (-0.5)
    return jnp.clip(content_vectors, -12.0, 12.0).astype(jnp.bfloat16)


def set_ends(result, own_key, low, top_value):
    index_at = [jax.random.randint(jax.random.fold_in(own_key, axis), (), 0, length) for axis, length in enumerate(result.shape)]
    widest = result.shape.index(max(result.shape))
    neighbour = index_at[:widest] + [(index_at[widest] + 1) % result.shape[widest]] + index_at[widest + 1:]
    return result.at[tuple(index_at)].set(low).at[tuple(neighbour)].set(top_value)


def level_of(key, dims, cuts, low, top_value):
    def one(dim, parts):
        heights = jax.random.uniform(jax.random.fold_in(jax.random.fold_in(key, 6), dim), (parts,), jnp.float32, low / len(cuts), top_value / len(cuts))
        return jnp.repeat(jnp.exp(heights), dims[dim] // parts).reshape((-1,) + (1,) * (len(dims) - dim - 1))

    level = one(*cuts[0])
    for cut in cuts[1:]:
        level = level * one(*cut)
    return level


def cumulative_ranks(amount, lean):
    portions = [(1 << 20) // math.isqrt(rank ** lean) + 1 for rank in range(1, amount + 1)]
    width = 1 + sum(portions) // (1 << 30)
    return np.cumsum(np.array([max(1, weight // width) for weight in portions]))


def ranked_ids(own_key, extent, amount, skew):
    grid = cumulative_ranks(amount, skew)
    ticket = jax.random.randint(jax.random.fold_in(own_key, 1), extent, 0, int(grid[amount - 1]))
    rank = jnp.searchsorted(jnp.asarray(grid, jnp.int32), ticket, side="right")
    return jax.random.permutation(jax.random.fold_in(own_key, 2), amount)[rank].astype(jnp.int32)


def noise(rng, shape, scale, limit, pieces=(), held_as=jnp.bfloat16):
    level = level_of(rng, shape, pieces, -0.22, 0.18) if pieces else 1.0
    array = jax.random.normal(rng, shape, jnp.float32) * scale * level
    return jnp.minimum(jnp.maximum(array, -limit), limit).astype(held_as)


def setup_inputs(seed: int = 0) -> dict:
    seeds = jax.random.split(jax.random.key(seed), 13)
    return {
        "incoming_homolog_features": noise(seeds[0], (HOMOLOG_TOTAL, CHAIN_LENGTH, FEATURE_DEPTH), 1.0, 6.0, ((0, 32), (1, 32))),
        "alignment_token_index": set_ends(ranked_ids(seeds[1], (HOMOLOG_TOTAL, CHAIN_LENGTH), SYMBOL_KINDS, 2), jax.random.fold_in(seeds[1], 3), 0, SYMBOL_KINDS - 1).astype(jnp.int32),
        "sequence_mask": set_ends((jax.random.randint(seeds[2], (HOMOLOG_TOTAL,), 0, 4) < 3).astype(jnp.int32), jax.random.fold_in(seeds[2], 1), 0, 1),
        "symbol_vector_lookup": noise(seeds[3], (SYMBOL_KINDS, FEATURE_DEPTH), 1.0, 6.0),
        "query_weight": draw_query_weight(jax.random.fold_in(seeds[12], 71), 0),
        "lookup_label_matrix": noise(seeds[5], (FEATURE_DEPTH, HEAD_NUMBER * SUBSPACE_SIZE), FEATURE_DEPTH ** -0.5, 0.375),
        "content_matrix": noise(seeds[6], (FEATURE_DEPTH, HEAD_NUMBER * SUBSPACE_SIZE), FEATURE_DEPTH ** -0.5, 0.375),
        "sigmoid_switch_matrix": noise(seeds[7], (FEATURE_DEPTH, HEAD_NUMBER * SUBSPACE_SIZE), FEATURE_DEPTH ** -0.5, 0.375),
        "final_mixing_matrix": noise(seeds[8], (HEAD_NUMBER * SUBSPACE_SIZE, FEATURE_DEPTH), (HEAD_NUMBER * SUBSPACE_SIZE) ** -0.5, 0.375),
        "first_operand_matrix": noise(seeds[9], (FEATURE_DEPTH, PRODUCT_DEPTH), FEATURE_DEPTH ** -0.5, 0.375),
        "second_operand_matrix": noise(seeds[10], (FEATURE_DEPTH, PRODUCT_DEPTH), FEATURE_DEPTH ** -0.5, 0.375),
        "pair_weight": noise(seeds[11], (PRODUCT_DEPTH * PRODUCT_DEPTH, CZ), (PRODUCT_DEPTH * PRODUCT_DEPTH // HOMOLOG_TOTAL) ** -0.5, 4.0),
    }


epsilon = 1e-05

def standardize_features(rows):
    average = lax.optimization_barrier(jnp.mean(rows, axis=-1, keepdims=True))
    centred = rows - average
    variance = lax.optimization_barrier(jnp.mean(centred * centred, axis=-1, keepdims=True))
    return centred * lax.rsqrt(variance + epsilon)

def attend_column(column, real_sequence_rows, query_weight, lookup_label_matrix, content_matrix, sigmoid_switch_matrix, final_mixing_matrix):
    standardized_features = standardize_features(column.astype(jnp.float32)).astype(jnp.bfloat16)

    def project(weight):
        return jnp.dot(standardized_features, weight, preferred_element_type=jnp.float32).astype(jnp.bfloat16).reshape(-1, HEAD_NUMBER, SUBSPACE_SIZE)
    query_rows = project(query_weight)
    key_rows = project(lookup_label_matrix)
    value_rows = project(content_matrix)
    gate_rows = project(sigmoid_switch_matrix)
    scores = jnp.einsum('shd,thd->hst', query_rows.astype(jnp.float32), key_rows.astype(jnp.float32))
    scores = scores * SUBSPACE_SIZE ** (-0.5) + (real_sequence_rows - 1.0) * 1000000000.0
    softmaxed = jax.nn.softmax(scores, axis=-1).astype(jnp.bfloat16)
    context = jnp.einsum('hst,thd->shd', softmaxed.astype(jnp.float32), value_rows.astype(jnp.float32))
    gated_values = (jax.nn.sigmoid(gate_rows.astype(jnp.float32)) * context).astype(jnp.bfloat16)
    gated_values = gated_values.reshape(-1, HEAD_NUMBER * SUBSPACE_SIZE)
    update = jnp.dot(gated_values, final_mixing_matrix, preferred_element_type=jnp.float32)
    return (column.astype(jnp.float32) + update).astype(jnp.bfloat16)

def reference(incoming_homolog_features, alignment_token_index, sequence_mask, symbol_vector_lookup, query_weight, lookup_label_matrix, content_matrix, sigmoid_switch_matrix, final_mixing_matrix, first_operand_matrix, second_operand_matrix, pair_weight):
    token_class_count = symbol_vector_lookup.shape[0]
    token_indicator = (alignment_token_index[:, :, None] == jnp.arange(token_class_count, dtype=jnp.int32)).astype(jnp.float32)
    token_embedding_rows = jnp.einsum('srv,vc->src', token_indicator, symbol_vector_lookup.astype(jnp.float32))
    alignment_state = (incoming_homolog_features.astype(jnp.float32) + token_embedding_rows).astype(jnp.bfloat16)
    real_sequence_rows = jnp.maximum(sequence_mask, (jnp.arange(HOMOLOG_TOTAL, dtype=jnp.int32) == 0).astype(jnp.int32)).astype(jnp.float32)
    live_count = jnp.sum(real_sequence_rows) + 0.001
    column_values = jnp.transpose(alignment_state, (1, 0, 2))
    updated_state = lax.map(lambda column: attend_column(column, real_sequence_rows, query_weight, lookup_label_matrix, content_matrix, sigmoid_switch_matrix, final_mixing_matrix), column_values)
    revised_homolog_features = jnp.transpose(updated_state, (1, 0, 2))
    standardized_features = standardize_features(revised_homolog_features.astype(jnp.float32)).astype(jnp.bfloat16).reshape(-1, FEATURE_DEPTH)
    left_factor = jnp.dot(standardized_features, first_operand_matrix, preferred_element_type=jnp.float32).reshape(HOMOLOG_TOTAL, CHAIN_LENGTH, PRODUCT_DEPTH)
    left_factor = (left_factor * real_sequence_rows[:, None, None]).astype(jnp.bfloat16)
    right_factor = jnp.dot(standardized_features, second_operand_matrix, preferred_element_type=jnp.float32).reshape(HOMOLOG_TOTAL, CHAIN_LENGTH, PRODUCT_DEPTH)
    right_factor = (right_factor * real_sequence_rows[:, None, None]).astype(jnp.bfloat16)
    right_flat = right_factor.reshape(HOMOLOG_TOTAL, CHAIN_LENGTH * PRODUCT_DEPTH)

    def pair_block(first_index):
        left_part = lax.dynamic_slice_in_dim(left_factor, first_index, RES_DEV, 1).reshape(HOMOLOG_TOTAL, RES_DEV * PRODUCT_DEPTH)
        outer_sum = jnp.dot(left_part.T, right_flat, preferred_element_type=jnp.float32).astype(jnp.bfloat16)
        outer_sum = outer_sum.reshape(RES_DEV, PRODUCT_DEPTH, CHAIN_LENGTH, PRODUCT_DEPTH).transpose(0, 2, 1, 3).reshape(RES_DEV * CHAIN_LENGTH, PRODUCT_DEPTH * PRODUCT_DEPTH)
        projected_values = jnp.dot(outer_sum, pair_weight, preferred_element_type=jnp.float32) / live_count
        return projected_values.reshape(RES_DEV, CHAIN_LENGTH, CZ)
    starts = jnp.arange(N_RES, dtype=jnp.int32) * RES_DEV
    pair = lax.map(pair_block, starts).reshape(CHAIN_LENGTH, CHAIN_LENGTH, CZ)
    pair_output = pair.reshape(CHAIN_LENGTH, N_RES, RES_DEV, CZ).transpose(0, 2, 1, 3)
    return (revised_homolog_features, pair_output)
```

```python
import functools
import math

import jax
import jax.numpy as jnp
from jax import lax
from jax.experimental import pallas as pl
from jax.experimental.pallas import tpu as pltpu
from jax.sharding import PartitionSpec as P

MESH = pl.DeviceIdType.MESH
F32, BF16, I32 = jnp.float32, jnp.bfloat16, jnp.int32
HEADS, SUB, EPS = 8, 32, 1e-5
DIMS = (4, 8, 2, 8)


def standardize(rows):
    centred = rows - jnp.mean(rows, axis=-1, keepdims=True)
    variance = jnp.mean(centred * centred, axis=-1, keepdims=True)
    return centred * lax.rsqrt(variance + EPS)


def dot(a, b):
    return jnp.dot(a, b, preferred_element_type=F32)


def dot_nt(a, b):
    return lax.dot_general(a, b, (((1,), (1,)), ((), ())), preferred_element_type=F32)


def iota(shape, axis):
    return lax.broadcasted_iota(I32, shape, axis)


def one_hot(test):
    return jnp.where(test, 1.0, 0.0).astype(BF16)


def turned(w):
    return w.astype(F32).T.astype(BF16)


def kernel(
    dims, x_ref, tok_ref, mask_ref, table_ref, wq_ref, wk_ref, wv_ref, wg_ref, wo_ref, w1_ref, w2_ref, pw_ref,
    rev_ref, pair_ref,
    snd, col, snd2, back, lt, rt, q_t, k_s, v_t, g_t, ctx, bias, table_s, pw_s, w4, wt, outer, lhs,
    a_send, a_recv, b_send, b_recv, l_send, r_send, y_sem, l_sem, n_sem, r_sem, c_sem,
):
    yh_n, z_n, yl_n, x_n = dims
    ns, nr = yh_n * z_n, yl_n * x_n * 2
    rows = x_ref.shape[0]
    sl = rows // ns
    block = min(256, rows)
    me_s, me_r = lax.axis_index("seq"), lax.axis_index("res")
    yh, z = lax.div(me_s, z_n), lax.rem(me_s, z_n)
    core, x, yl = lax.rem(me_r, 2), lax.rem(lax.div(me_r, 2), x_n), lax.div(me_r, 2 * x_n)

    def res_id(yl_, x_, core_):
        return (yl_ * x_n + x_) * 2 + core_

    def seq_id(b, dz):
        return lax.rem(yh + b, yh_n) * z_n + lax.rem(z + dz + z_n, z_n)

    def res_of(b, dx, core_):
        return res_id(lax.rem(yl + b, yl_n), lax.rem(x + dx + x_n, x_n), core_)

    barrier = pltpu.get_barrier_semaphore()

    def greet(off, carry):
        pl.semaphore_signal(barrier, inc=1, device_id=(lax.rem(me_s + off, ns), me_r), device_id_type=MESH)
        return carry

    lax.fori_loop(1, ns, greet, 0)
    for peer in (res_of(0, 0, 1 - core), res_of(1, 0, core), res_of(0, 1, core), res_of(0, -1, core)):
        pl.semaphore_signal(barrier, inc=1, device_id=(me_s, peer), device_id_type=MESH)

    n_rows = iota((rows, rows), 0)
    sl_bits, ns_bits = sl.bit_length() - 1, ns.bit_length() - 1
    pick = one_hot(iota((rows, rows), 1) == (n_rows & (sl - 1)) * ns + (n_rows >> sl_bits))
    n_seq = iota((rows, sl), 0) & (sl - 1)
    token_rows = dot(one_hot(iota((rows, sl), 1) == n_seq), tok_ref[...].astype(F32).astype(BF16))
    own = (iota((rows, ns), 0) >> sl_bits) == iota((rows, ns), 1)
    token = jnp.sum(jnp.where(own, token_rows, 0.0), axis=1, keepdims=True)
    kinds = table_ref.shape[0]
    table_s[...] = jnp.zeros_like(table_s)
    table_s[0:kinds, :] = table_ref[...].astype(F32)
    classes = table_s.shape[0]
    token_hot = one_hot(iota((rows, classes), 1).astype(F32) == token)
    msa = (dot(pick, x_ref[...]) + dot(token_hot, table_s[...].astype(BF16))).astype(BF16)
    snd[...] = msa.reshape(snd.shape)
    col[pl.ds(me_s, 1)] = snd[pl.ds(me_s, 1)]

    pl.semaphore_wait(barrier, ns - 1 + 4)

    def send_out(off, carry):
        to = lax.rem(me_s + off, ns)
        pltpu.make_async_remote_copy(
            src_ref=snd.at[to], dst_ref=col.at[me_s], send_sem=a_send, recv_sem=a_recv,
            device_id=(to, me_r), device_id_type=MESH,
        ).start()
        return carry

    lax.fori_loop(1, ns, send_out, 0)

    wt[0:256, :] = turned(wq_ref[...])
    wt[256:512, :] = turned(wv_ref[...])
    wt[512:768, :] = turned(wg_ref[...])
    wt[768:800, :] = turned(w1_ref[...])
    wt[800:832, :] = turned(w2_ref[...])
    live = jnp.where(iota((1, rows), 1) == 0, 1, mask_ref[...]).astype(F32)
    live_col = jnp.sum(jnp.where(n_rows == iota((rows, rows), 1), live, 0.0), axis=1, keepdims=True)
    bias[...] = jnp.broadcast_to((live_col - 1.0) * 1e9, bias.shape)
    count = jnp.sum(live, axis=1, keepdims=True) + 0.001
    pw_s[...] = pw_ref[...].astype(F32)
    w4[...] = jnp.zeros_like(w4)

    def spread(e, carry):
        part = pw_s[pl.ds(e, 32, stride=32), :].astype(BF16)
        for i in range(4):
            w4[pl.ds(pl.multiple_of(e * 128 + i * 32, 32), 32), i * 128 : (i + 1) * 128] = part
        return carry

    lax.fori_loop(0, 32, spread, 0)

    pltpu.make_async_copy(snd.at[pl.ds(0, ns - 1)], col.at[pl.ds(0, ns - 1)], a_recv).wait()

    column = col[...].reshape(rows, 256).astype(F32)
    normed = standardize(column).astype(BF16)
    k_s[...] = dot(normed, wk_ref[...]).astype(BF16)
    q_t[...] = dot_nt(wt[0:256, :], normed).astype(BF16).astype(F32)
    v_t[...] = dot_nt(wt[256:512, :], normed).astype(BF16)
    g_t[...] = jax.nn.sigmoid(dot_nt(wt[512:768, :], normed).astype(BF16).astype(F32))
    factor = SUB**-0.5 * math.log2(math.e)

    def head(h, carry):
        at = pl.multiple_of(lax.div(h, 4) * 128, 128)
        here = pl.multiple_of(h * SUB, SUB)
        keys = k_s[:, pl.ds(at, 128)]
        query = jnp.where((iota((128, rows), 0) >> 5) == lax.rem(h, 4), q_t[pl.ds(at, 128), :], 0.0).astype(BF16)
        values = v_t[pl.ds(here, SUB), :]
        for b in range(rows // block):
            part = slice(b * block, (b + 1) * block)
            scores = dot(keys, query[:, part]) + bias[...]
            top = jnp.max(scores, axis=0, keepdims=True)
            weights = jnp.exp2((scores - top) * factor)
            total = jnp.sum(weights, axis=0, keepdims=True)
            ctx[pl.ds(here, SUB), part] = dot(values, weights.astype(BF16)) / total
        return carry

    lax.fori_loop(0, HEADS, head, 0)
    gated = (g_t[...] * ctx[...]).T.astype(BF16)
    revised = (column + dot(gated, wo_ref[...])).astype(BF16)
    snd2[...] = revised.reshape(snd2.shape)
    back[pl.ds(me_s, 1)] = snd2[pl.ds(me_s, 1)]
    normed = standardize(revised.astype(F32)).astype(BF16)
    factors = (dot_nt(wt[768:832, :], normed) * live).astype(BF16)
    lt[pl.ds(me_s, 1)] = factors[0:32].reshape(1, 32, rows)
    rt[pl.ds(me_r, 1)] = factors[32:64].reshape(1, 32, rows)

    def part_of(buf, at, half):
        return buf.at[at] if half is None else buf.at[at, pl.ds(16 * half, 16)]

    def push(buf, at, dev, send, recv, half=None):
        ref = part_of(buf, at, half)
        pltpu.make_async_remote_copy(
            src_ref=ref, dst_ref=ref, send_sem=send, recv_sem=recv, device_id=dev, device_id_type=MESH
        ).start()

    def arrived(buf, at, recv, half=None):
        ref = part_of(buf, at, half)
        pltpu.make_async_copy(ref, ref, recv).wait()

    def ring(buf, n, index, device, send, sems):
        far = n // 2

        def give(b, way, k):
            step = 1 - 2 * way
            half = way if k + 1 == far else None
            push(buf, index(b, -step * k), device(step), send, sems.at[(b * 2 + way) * far + k], half)

        def take(b, way, k):
            step = 1 - 2 * way
            half = way if k == far else None
            arrived(buf, index(b, -step * k), sems.at[(b * 2 + way) * far + k - 1], half)

        return far, give, take

    l_far, l_give, l_take = ring(lt, z_n, seq_id, lambda s: (seq_id(0, s), me_r), l_send, l_sem)
    r_far, r_give, r_take = ring(
        rt, x_n, lambda b, d: res_of(b, d, core), lambda s: (me_s, res_of(0, s, core)), r_send, r_sem
    )
    mate = (me_s, res_of(0, 0, 1 - core))

    def hand_over(b, dx):
        push(rt, res_of(b, dx, core), mate, r_send, c_sem.at[b * x_n + dx % x_n])

    for way in range(2):
        l_give(0, way, 0)
        r_give(0, way, 0)
    push(rt, me_r, (me_s, res_of(1, 0, core)), r_send, n_sem)
    for b in range(1, yh_n):
        push(lt, me_s, (seq_id(b, 0), me_r), l_send, y_sem.at[yh_n - b - 1])
    hand_over(0, 0)

    def send_back(off, carry):
        to = lax.rem(me_s + off, ns)
        pltpu.make_async_remote_copy(
            src_ref=snd2.at[to], dst_ref=back.at[me_s], send_sem=b_send, recv_sem=b_recv,
            device_id=(to, me_r), device_id_type=MESH,
        ).start()
        return carry

    lax.fori_loop(1, ns, send_back, 0)

    def r_step(k):
        for b in range(2):
            for way in range(2):
                r_take(b, way, k)
                if k < r_far:
                    r_give(b, way, k)
                    hand_over(b, k * (2 * way - 1))
            if k == r_far:
                hand_over(b, k)

    def l_step(k):
        for b in range(yh_n):
            for way in range(2):
                l_take(b, way, k)
                if k < l_far:
                    l_give(b, way, k)

    arrived(rt, res_of(1, 0, core), n_sem)
    for way in range(2):
        r_give(1, way, 0)
    hand_over(1, 0)
    for b in range(1, yh_n):
        arrived(lt, seq_id(b, 0), y_sem.at[b - 1])
        for way in range(2):
            l_give(b, way, 0)
    for k in range(1, max(r_far, l_far) + 1):
        if k <= r_far:
            r_step(k)
        if k <= l_far:
            l_step(k)
    for b in range(2):
        for dx in range(x_n):
            arrived(rt, res_of(b, dx, 1 - core), c_sem.at[b * x_n + dx])

    right = rt[...].reshape(nr * 32, rows)
    wide = min(256, ns * 32)
    tiles = wide // 128

    def outer_part(n, carry):
        left = lt[pl.ds(n * (wide // 32), wide // 32)].reshape(wide, rows)
        product = dot_nt(right, left)
        for t in range(tiles):
            outer[n * tiles + t] = product[:, t * 128 : (t + 1) * 128]
        return carry

    lax.fori_loop(0, ns * 32 // wide, outer_part, 0)

    def gather_part(e, carry):
        at = pl.multiple_of(e * 128, 128)
        for g in range(ns // 4):
            part = outer[g, pl.ds(e, nr, stride=32), :]
            lhs[g * nr : (g + 1) * nr, pl.ds(at, 128)] = part.astype(BF16)
        return carry

    lax.fori_loop(0, 32, gather_part, 0)
    pair = dot(lhs[...], w4[...]) / count
    for g in range(ns // 4):
        for i in range(4):
            pair_ref[4 * g + i] = pair[g * nr : (g + 1) * nr, i * 128 : (i + 1) * 128]

    pltpu.make_async_copy(snd2.at[pl.ds(0, ns - 1)], back.at[pl.ds(0, ns - 1)], b_recv).wait()
    unpick = one_hot(iota((rows, rows), 1) == (n_rows & (ns - 1)) * sl + (n_rows >> ns_bits))
    rev_ref[...] = dot(unpick, back[...].reshape(rows, 256)).astype(BF16)

    pltpu.make_async_copy(snd.at[pl.ds(0, ns - 1)], snd.at[pl.ds(0, ns - 1)], a_send).wait()
    pltpu.make_async_copy(snd2.at[pl.ds(0, ns - 1)], snd2.at[pl.ds(0, ns - 1)], b_send).wait()
    pltpu.make_async_copy(lt.at[pl.ds(0, ns - 1)], lt.at[pl.ds(0, ns - 1)], l_send).wait()
    pltpu.make_async_copy(rt.at[pl.ds(0, nr - 1)], rt.at[pl.ds(0, nr - 1)], r_send).wait()


def per_device(dims, features, tokens, mask, table, wq, wk, wv, wg, wo, w1, w2, pw):
    yh_n, z_n, yl_n, x_n = dims
    ns, nr = yh_n * z_n, yl_n * x_n * 2
    sl, res_local, width = features.shape
    rows = sl * res_local
    block = min(256, rows)
    vmem = pl.BlockSpec(memory_space=pltpu.VMEM)
    dma = pltpu.SemaphoreType.DMA
    revised, pair = pl.pallas_call(
        functools.partial(kernel, dims),
        out_shape=(
            jax.ShapeDtypeStruct((rows, width), BF16),
            jax.ShapeDtypeStruct((ns, nr, pw.shape[1]), F32),
        ),
        in_specs=[vmem] * 12,
        out_specs=(vmem, vmem),
        scratch_shapes=[
            pltpu.VMEM((ns, sl, width), BF16),
            pltpu.VMEM((ns, sl, width), BF16),
            pltpu.VMEM((ns, sl, width), BF16),
            pltpu.VMEM((ns, sl, width), BF16),
            pltpu.VMEM((ns, 32, rows), BF16),
            pltpu.VMEM((nr, 32, rows), BF16),
            pltpu.VMEM((256, rows), F32),
            pltpu.VMEM((rows, 256), BF16),
            pltpu.VMEM((256, rows), BF16),
            pltpu.VMEM((256, rows), F32),
            pltpu.VMEM((256, rows), F32),
            pltpu.VMEM((rows, block), F32),
            pltpu.VMEM((32, width), F32),
            pltpu.VMEM(pw.shape, F32),
            pltpu.VMEM((32 * 128, 512), BF16),
            pltpu.VMEM((832, 256), BF16),
            pltpu.VMEM((ns // 4, nr * 32, 128), F32),
            pltpu.VMEM((ns // 4 * nr, 32 * 128), BF16),
            dma, dma, dma, dma, dma, dma,
            dma((yh_n - 1,)),
            dma((yh_n * z_n,)),
            dma,
            dma((yl_n * x_n,)),
            dma((yl_n * x_n,)),
        ],
        compiler_params=pltpu.CompilerParams(collective_id=0, has_side_effects=True),
    )(
        features.reshape(rows, width), tokens, mask.reshape(1, -1), table,
        wq, wk, wv, wg, wo, w1, w2, pw,
    )
    return revised.reshape(features.shape), pair.reshape(ns, 1, nr, pw.shape[1])


def solution(mesh, dims=DIMS):
    return jax.shard_map(
        functools.partial(per_device, dims),
        mesh=mesh,
        in_specs=(P("seq", "res", None), P("seq", "res")) + (P(),) * 10,
        out_specs=(P("seq", "res", None), P("res", "seq", None, None)),
        check_vma=False,
    )
```

```python
import functools
import math

import jax
import jax.numpy as jnp
from jax import lax
from jax.experimental import pallas as pl
from jax.experimental.pallas import tpu as pltpu
from jax.sharding import PartitionSpec as P

MESH = pl.DeviceIdType.MESH
F32, BF16, I32 = jnp.float32, jnp.bfloat16, jnp.int32
HEADS, SUB, EPS = 8, 32, 1e-5
DIMS = (4, 8, 2, 8)
VMEM_BYTES = 36 << 20
SCHEDULE = (
    "r", "s", "c", "L01", "R01", "N", "B2", "Y1", "Y3", "Y2", "B2", "L02", "R02", "R11",
    "L11", "L31", "L21", "B4", "L03", "R03", "R12", "L12", "L32", "L22", "B4", "R04", "R13", "L13",
    "L33", "L23", "B4", "R14", "P", "O1", "O2", "O3", "L04", "L14", "L34", "L24", "O4",
)


def standardize(rows):
    centred = rows - jnp.mean(rows, axis=-1, keepdims=True)
    variance = jnp.mean(centred * centred, axis=-1, keepdims=True)
    return centred * lax.rsqrt(variance + EPS)


def dot(a, b):
    return jnp.dot(a, b, preferred_element_type=F32)


def dot_nt(a, b):
    return lax.dot_general(a, b, (((1,), (1,)), ((), ())), preferred_element_type=F32)


def iota(shape, axis):
    return lax.broadcasted_iota(I32, shape, axis)


def one_hot(test):
    return jnp.where(test, 1.0, 0.0).astype(BF16)


def turned(w):
    return w.astype(F32).T.astype(BF16)


def kernel(
    dims, x_h, tok_h, mask_h, table_h, wq_h, wk_h, wv_h, wg_h, wo_h, w1_h, w2_h, pw_h,
    rev_ref, pair_ref,
    x_ref, tok_ref, mask_ref, table_ref, wq_ref, wk_ref, wv_ref, wg_ref, wo_ref, pw_ref,
    snd, col, snd2, back, lt, rt, q_t, k_s, v_t, g_t, ctx, bias, table_s, pw_s, w4, wt, perm, rp, fac, lhs,
    in_sem, a_send, a_recv, b_send, b_recv, l_send, r_send, y_sem, l_sem, n_sem, r_sem, c_sem,
):
    yh_n, z_n, yl_n, x_n = dims
    ns, nr = yh_n * z_n, yl_n * x_n * 2
    half_n, zh_n = ns // 2, z_n // 2
    rows = x_ref.shape[0]
    sl = rows // ns
    block = rows // 2
    me_s, me_r = lax.axis_index("seq"), lax.axis_index("res")
    yh, z = lax.div(me_s, z_n), lax.rem(me_s, z_n)
    core, x, yl = lax.rem(me_r, 2), lax.rem(lax.div(me_r, 2), x_n), lax.div(me_r, 2 * x_n)
    zh = lax.div(z, 2)
    slot = lax.rem(z, 2) * half_n + yh * zh_n + zh

    def seq_id(b, dz):
        return lax.rem(yh + b, yh_n) * z_n + lax.rem(z + dz + z_n, z_n)

    def left_at(b, dz):
        return lax.rem(z + dz + z_n, z_n) * yh_n + lax.rem(yh + b, yh_n)

    def res_of(b, dx, core_):
        return (lax.rem(yl + b, yl_n) * x_n + lax.rem(x + dx + x_n, x_n)) * 2 + core_

    loads = [
        pltpu.make_async_copy(src, dst, in_sem.at[i])
        for i, (src, dst) in enumerate((
            (tok_h, tok_ref), (table_h, table_ref), (x_h, x_ref), (mask_h, mask_ref), (wq_h, wq_ref), (wk_h, wk_ref), (wv_h, wv_ref), (wg_h, wg_ref), (wo_h, wo_ref),
            (w1_h, wt.at[pl.ds(768, 32)]), (w2_h, wt.at[pl.ds(800, 32)]), (pw_h, pw_ref),
        ))
    ]
    for load in loads[:3]:
        load.start()

    barrier = pltpu.get_barrier_semaphore()

    def greet(off, carry):
        pl.semaphore_signal(barrier, inc=1, device_id=(lax.rem(me_s + off, ns), me_r), device_id_type=MESH)
        return carry

    lax.fori_loop(1, ns, greet, 0)
    for peer in (res_of(0, 0, 1 - core), res_of(1, 0, core), res_of(0, 1, core), res_of(0, -1, core)):
        pl.semaphore_signal(barrier, inc=1, device_id=(me_s, peer), device_id_type=MESH)
    for load in loads[3:]:
        load.start()

    n_rows = iota((rows, rows), 0)
    n_cols = iota((rows, rows), 1)
    sl_bits, ns_bits = sl.bit_length() - 1, ns.bit_length() - 1
    pick = one_hot(n_cols == (n_rows & (sl - 1)) * ns + (n_rows >> sl_bits))
    loads[0].wait()
    loads[1].wait()
    n_seq = iota((rows, sl), 0) & (sl - 1)
    token_rows = dot(one_hot(iota((rows, sl), 1) == n_seq), tok_ref[...].astype(F32).astype(BF16))
    own = (iota((rows, ns), 0) >> sl_bits) == iota((rows, ns), 1)
    token = jnp.sum(jnp.where(own, token_rows, 0.0), axis=1, keepdims=True)
    kinds = table_ref.shape[0]
    table_s[...] = jnp.zeros_like(table_s)
    table_s[0:kinds, :] = table_ref[...].astype(F32)
    classes = table_s.shape[0]
    token_hot = one_hot(iota((rows, classes), 1).astype(F32) == token)
    embedded = dot(token_hot, table_s[...].astype(BF16))
    loads[2].wait()
    msa = (dot(pick, x_ref[...]) + embedded).astype(BF16)
    snd[...] = msa.reshape(snd.shape)
    col[pl.ds(slot, 1)] = snd[pl.ds(me_s, 1)]

    pl.semaphore_wait(barrier, ns - 1 + 4)

    def send_out(t, carry):
        off = lax.rem(t * 11, ns)
        to = lax.rem(yh + lax.div(off, z_n), yh_n) * z_n + lax.rem(z + lax.rem(off, z_n), z_n)
        pltpu.make_async_remote_copy(
            src_ref=snd.at[to], dst_ref=col.at[slot], send_sem=a_send, recv_sem=a_recv,
            device_id=(to, me_r), device_id_type=MESH,
        ).start()
        return carry

    lax.fori_loop(1, ns, send_out, 0)

    for load in loads[3:]:
        load.wait()
    wt[0:256, :] = turned(wq_ref[...])
    wt[256:512, :] = turned(wv_ref[...])
    wt[512:768, :] = turned(wg_ref[...])
    live_all = jnp.where(iota((16, rows), 1) == 0, 1, mask_ref[...]).astype(F32)
    count = jnp.sum(live_all[0:1], axis=1, keepdims=True) + 0.001
    place = n_cols >> sl_bits
    spot = place & (half_n - 1)
    zh_bits = zh_n.bit_length() - 1
    device = (spot >> zh_bits) * z_n + (spot & (zh_n - 1)) * 2 + jnp.where(place >= half_n, 1, 0)
    order = one_hot(n_rows == device * sl + (n_cols & (sl - 1)))
    live = dot(live_all.astype(BF16), order)[0:1]
    live_col = jnp.sum(jnp.where(n_rows == n_cols, live, 0.0), axis=1, keepdims=True)
    bias[...] = jnp.broadcast_to((live_col - 1.0) * 1e9, bias.shape)
    wide = nr * 32
    turn = iota((256, 256), 0)
    perm[...] = one_hot(iota((256, 256), 1) == (turn & 7) * 32 + (turn >> 3))
    pw_s[...] = pw_ref[...].astype(F32)
    w4[...] = jnp.zeros_like(w4)

    def spread(e, carry):
        part = pw_s[pl.ds(e, 32, stride=32), :].astype(BF16)
        for i in range(4):
            w4[pl.ds(pl.multiple_of(e * 128 + i * 32, 32), 32), i * 128 : (i + 1) * 128] = part
        return carry

    lax.fori_loop(0, 32, spread, 0)

    pltpu.make_async_copy(snd.at[pl.ds(0, ns - 1)], col.at[pl.ds(0, ns - 1)], a_recv).wait()

    normed = standardize(col[...].reshape(rows, 256).astype(F32)).astype(BF16)
    k_s[...] = dot(normed, wk_ref[...]).astype(BF16)
    q_t[...] = dot_nt(wt[0:256, :], normed).astype(BF16).astype(F32)
    v_t[...] = dot_nt(wt[256:512, :], normed).astype(BF16)
    g_t[...] = jax.nn.sigmoid(dot_nt(wt[512:768, :], normed).astype(BF16).astype(F32))
    factor = SUB**-0.5 * math.log2(math.e)

    def one_head(h, part):
        at = pl.multiple_of(lax.div(h, 4) * 128, 128)
        here = pl.multiple_of(h * SUB, SUB)
        query = jnp.where((iota((128, block), 0) >> 5) == lax.rem(h, 4), q_t[pl.ds(at, 128), part], 0.0).astype(BF16)
        scores = dot(k_s[:, pl.ds(at, 128)], query) + bias[...]
        top = jnp.max(scores, axis=0, keepdims=True)
        weights = jnp.exp2((scores - top) * factor)
        total = jnp.sum(weights, axis=0, keepdims=True)
        ctx[pl.ds(here, SUB), part] = dot(v_t[pl.ds(here, SUB), :], weights.astype(BF16)) / total

    def attend(b):
        part = slice(b * block, (b + 1) * block)

        def heads(h, carry):
            for j in range(2):
                one_head(h * 2 + j, part)
            return carry

        lax.fori_loop(0, HEADS // 2, heads, 0)
        gated = (g_t[:, part] * ctx[:, part]).T.astype(BF16)
        column = col[b * half_n : (b + 1) * half_n].reshape(block, 256).astype(F32)
        revised = (column + dot(gated, wo_ref[...])).astype(BF16)
        snd2[b * half_n : (b + 1) * half_n] = revised.reshape(half_n, sl, 256)
        again = standardize(revised.astype(F32)).astype(BF16)
        fac[:, part] = (dot_nt(wt[768:832, :], again) * live[:, part]).astype(BF16)

    def send_back(b, first, last):
        def one(t, carry):
            off = lax.rem(t * 5, half_n)
            to_y = lax.rem(yh + lax.div(off, zh_n), yh_n)
            to_z = lax.rem(zh + lax.rem(off, zh_n), zh_n)
            to = to_y * z_n + to_z * 2 + b

            @pl.when(to != me_s)
            def _():
                pltpu.make_async_remote_copy(
                    src_ref=snd2.at[b * half_n + to_y * zh_n + to_z], dst_ref=back.at[me_s],
                    send_sem=b_send, recv_sem=b_recv, device_id=(to, me_r), device_id_type=MESH,
                ).start()

            return carry

        lax.fori_loop(first, last, one, 0)

    def part_of(buf, at, half):
        return buf.at[at] if half is None else buf.at[at, pl.ds(16 * half, 16)]

    def push(buf, at, dev, send, recv, half=None):
        ref = part_of(buf, at, half)
        pltpu.make_async_remote_copy(
            src_ref=ref, dst_ref=ref, send_sem=send, recv_sem=recv, device_id=dev, device_id_type=MESH
        ).start()

    def arrived(buf, at, recv, half=None):
        ref = part_of(buf, at, half)
        pltpu.make_async_copy(ref, ref, recv).wait()

    def ring(buf, n, index, device, send, sems):
        far = n // 2

        def give(b, way, k):
            step = 1 - 2 * way
            half = way if k + 1 == far else None
            push(buf, index(b, -step * k), device(step), send, sems.at[(b * 2 + way) * far + k], half)

        def take(b, way, k):
            step = 1 - 2 * way
            half = way if k == far else None
            arrived(buf, index(b, -step * k), sems.at[(b * 2 + way) * far + k - 1], half)

        return far, give, take

    l_far, l_give, l_take = ring(lt, z_n, left_at, lambda s: (seq_id(0, s), me_r), l_send, l_sem)
    r_far, r_give, r_take = ring(
        rt, x_n, lambda b, d: res_of(b, d, core), lambda s: (me_s, res_of(0, s, core)), r_send, r_sem
    )
    mate = (me_s, res_of(0, 0, 1 - core))

    def hand_over(b, dx):
        push(rt, res_of(b, dx, core), mate, r_send, c_sem.at[b * x_n + dx % x_n])

    def r_step(k):
        for b in range(2):
            for way in range(2):
                r_take(b, way, k)
                if k < r_far:
                    r_give(b, way, k)
                    hand_over(b, k * (2 * way - 1))
            if k == r_far:
                hand_over(b, k)

    def l_step(k):
        for b in range(yh_n):
            for way in range(2):
                l_take(b, way, k)
                if k < l_far:
                    l_give(b, way, k)

    attend(0)
    send_back(0, 0, half_n)
    attend(1)
    lt[pl.ds(left_at(0, 0), 1)] = fac[0:32, :].reshape(1, 32, rows)
    rt[pl.ds(me_r, 1)] = fac[32:64, :].reshape(1, 32, rows)
    back[pl.ds(me_s, 1)] = snd2[pl.ds(slot, 1)]

    def start_row():
        push(rt, me_r, (me_s, res_of(1, 0, core)), r_send, n_sem)

    def start_rings():
        for way in range(2):
            l_give(0, way, 0)
            r_give(0, way, 0)

    def start_columns():
        for b in range(1, yh_n):
            push(lt, left_at(0, 0), (seq_id(b, 0), me_r), l_send, y_sem.at[yh_n - b - 1])

    def next_row():
        arrived(rt, res_of(1, 0, core), n_sem)
        for way in range(2):
            r_give(1, way, 0)
        hand_over(1, 0)

    def next_column(b):
        arrived(lt, left_at(b, 0), y_sem.at[b - 1])
        for way in range(2):
            l_give(b, way, 0)

    def r_step(b, k):
        if 1 <= k <= r_far:
            for way in range(2):
                r_take(b, way, k)
                if k < r_far:
                    r_give(b, way, k)
                    hand_over(b, k * (2 * way - 1))
            if k == r_far:
                hand_over(b, k)

    def l_step(b, k):
        if 1 <= k <= l_far:
            for way in range(2):
                l_take(b, way, k)
                if k < l_far:
                    l_give(b, way, k)

    def right_rows():
        for b in range(2):
            for dx in range(x_n):
                arrived(rt, res_of(b, dx, 1 - core), c_sem.at[b * x_n + dx])
        for n in range(nr // 8):
            eight = rt[n * 8 : (n + 1) * 8].reshape(256, rows)
            rp[n * 256 : (n + 1) * 256, :] = dot(perm[...], eight).astype(BF16)

    groups = []

    def outer_part(*distances):
        lefts = []
        for dz in distances:
            group = lax.rem(z + dz + z_n, z_n)
            groups.append(group)
            lefts.append(lt[pl.ds(group * yh_n, yh_n)].reshape(yh_n * 32, rows))
        product = dot_nt(rp[...], jnp.concatenate(lefts, axis=0))
        for j in range(len(distances)):
            to = (len(groups) - len(distances) + j) * nr
            for e in range(32):
                lane = slice(j * 128, (j + 1) * 128)
                eights = [product[n * 256 + e * 8 : n * 256 + (e + 1) * 8, lane] for n in range(nr // 8)]
                lhs[to : to + nr, e * 128 : (e + 1) * 128] = jnp.concatenate(eights, axis=0).astype(BF16)

    sent = 0
    for word in SCHEDULE:
        kind, args = word[0], [int(c) for c in word[1:]]
        if kind == "r":
            start_row()
            hand_over(0, 0)
        elif kind == "s":
            start_rings()
        elif kind == "c":
            start_columns()
        elif kind == "N":
            next_row()
        elif kind == "Y":
            next_column(*args)
        elif kind == "R":
            r_step(*args)
        elif kind == "L":
            l_step(*args)
        elif kind == "P":
            right_rows()
        elif kind == "B":
            more = min(args[0], half_n - sent)
            send_back(1, sent, sent + more)
            sent += more
        elif kind == "O":
            if args[0] < l_far:
                outer_part(-args[0], args[0])
            elif args[0] == l_far:
                outer_part(0, l_far)

    pair = dot(lhs[...], w4[...]) / count
    for n, group in enumerate(groups):
        for i in range(4):
            pair_ref[i * z_n + group] = pair[n * nr : (n + 1) * nr, i * 128 : (i + 1) * 128]

    pltpu.make_async_copy(snd2.at[pl.ds(0, ns - 1)], back.at[pl.ds(0, ns - 1)], b_recv).wait()
    unpick = one_hot(n_cols == (n_rows & (ns - 1)) * sl + (n_rows >> ns_bits))
    rev_ref[...] = dot(unpick, back[...].reshape(rows, 256)).astype(BF16)

    pltpu.make_async_copy(snd.at[pl.ds(0, ns - 1)], snd.at[pl.ds(0, ns - 1)], a_send).wait()
    pltpu.make_async_copy(snd2.at[pl.ds(0, ns - 1)], snd2.at[pl.ds(0, ns - 1)], b_send).wait()
    pltpu.make_async_copy(lt.at[pl.ds(0, ns - 1)], lt.at[pl.ds(0, ns - 1)], l_send).wait()
    pltpu.make_async_copy(rt.at[pl.ds(0, nr - 1)], rt.at[pl.ds(0, nr - 1)], r_send).wait()


def per_device(dims, features, tokens, mask, table, wq, wk, wv, wg, wo, w1, w2, pw):
    yh_n, z_n, yl_n, x_n = dims
    ns, nr = yh_n * z_n, yl_n * x_n * 2
    sl, res_local, width = features.shape
    rows = sl * res_local
    vmem, hbm = pl.BlockSpec(memory_space=pltpu.VMEM), pl.BlockSpec(memory_space=pltpu.HBM)
    dma = pltpu.SemaphoreType.DMA
    revised, pair = pl.pallas_call(
        functools.partial(kernel, dims),
        out_shape=(
            jax.ShapeDtypeStruct((rows, width), BF16),
            jax.ShapeDtypeStruct((ns, nr, pw.shape[1]), F32),
        ),
        in_specs=[hbm] * 12,
        out_specs=(vmem, vmem),
        scratch_shapes=[
            pltpu.VMEM((rows, width), BF16),
            pltpu.VMEM(tokens.shape, I32),
            pltpu.VMEM((1, rows), I32),
            pltpu.VMEM(table.shape, BF16),
            *[pltpu.VMEM((width, width), BF16)] * 5,
            pltpu.VMEM(pw.shape, BF16),
            *[pltpu.VMEM((ns, sl, width), BF16)] * 4,
            pltpu.VMEM((ns, 32, rows), BF16),
            pltpu.VMEM((nr, 32, rows), BF16),
            pltpu.VMEM((256, rows), F32),
            pltpu.VMEM((rows, 256), BF16),
            pltpu.VMEM((256, rows), BF16),
            pltpu.VMEM((256, rows), F32),
            pltpu.VMEM((256, rows), F32),
            pltpu.VMEM((rows, rows // 2), F32),
            pltpu.VMEM((32, width), F32),
            pltpu.VMEM(pw.shape, F32),
            pltpu.VMEM((32 * 128, 512), BF16),
            pltpu.VMEM((832, 256), BF16),
            pltpu.VMEM((256, 256), BF16),
            pltpu.VMEM((nr * 32, rows), BF16),
            pltpu.VMEM((64, rows), BF16),
            pltpu.VMEM((z_n * nr, 32 * 128), BF16),
            dma((12,)),
            dma, dma, dma, dma, dma, dma,
            dma((yh_n - 1,)),
            dma((yh_n * z_n,)),
            dma,
            dma((yl_n * x_n,)),
            dma((yl_n * x_n,)),
        ],
        compiler_params=pltpu.CompilerParams(
            collective_id=0, has_side_effects=True, vmem_limit_bytes=VMEM_BYTES
        ),
    )(
        *[
            pltpu.with_memory_space_constraint(a, pltpu.HBM)
            for a in (
                features.reshape(rows, width), tokens, mask.reshape(1, -1), table,
                wq, wk, wv, wg, wo, w1.T, w2.T, pw,
            )
        ]
    )
    return revised.reshape(features.shape), pair.reshape(ns, 1, nr, pw.shape[1])


def solution(mesh, dims=DIMS):
    return jax.shard_map(
        functools.partial(per_device, dims),
        mesh=mesh,
        in_specs=(P("seq", "res", None), P("seq", "res")) + (P(),) * 10,
        out_specs=(P("seq", "res", None), P("res", "seq", None, None)),
        check_vma=False,
    )
```

```python
import functools
import math

import jax
import jax.numpy as jnp
from jax import lax
from jax.experimental import pallas as pl
from jax.experimental.pallas import tpu as pltpu
from jax.sharding import PartitionSpec as P

MESH = pl.DeviceIdType.MESH
F32, BF16, I32 = jnp.float32, jnp.bfloat16, jnp.int32
HEADS, SUB, EPS = 8, 32, 1e-5
DIMS = (4, 8, 2, 8)
VMEM_BYTES = 36 << 20
SCHEDULE = (
    "r", "s", "c", "L01", "R01", "N", "B2", "Y1", "Y3", "Y2", "B2", "L02", "R02", "R11",
    "L11", "L31", "L21", "B4", "L03", "R03", "R12", "L12", "L32", "L22", "B4", "R04", "R13", "L13",
    "L33", "L23", "B4", "R14", "P", "O1", "O2", "O3", "L04", "L14", "L34", "L24", "O4",
)


def standardize(rows):
    centred = rows - jnp.mean(rows, axis=-1, keepdims=True)
    variance = jnp.mean(centred * centred, axis=-1, keepdims=True)
    return centred * lax.rsqrt(variance + EPS)


def dot(a, b):
    return jnp.dot(a, b, preferred_element_type=F32)


def dot_nt(a, b):
    return lax.dot_general(a, b, (((1,), (1,)), ((), ())), preferred_element_type=F32)


def iota(shape, axis):
    return lax.broadcasted_iota(I32, shape, axis)


def one_hot(test):
    return jnp.where(test, 1.0, 0.0).astype(BF16)


def turned(w):
    return w.astype(F32).T.astype(BF16)


def kernel(
    dims, x_h, tok_h, mask_h, table_h, wq_h, wk_h, wv_h, wg_h, wo_h, w1_h, w2_h, pw_h,
    rev_ref, pair_ref,
    x_ref, tok_ref, mask_ref, table_ref, wq_ref, wk_ref, wv_ref, wg_ref, wo_ref, pw_ref,
    snd, col, snd2, back, lt, rt, q_t, k_s, v_t, g_t, ctx, bias, table_s, pw_s, w4, wt, perm, rp, fac, lhs,
    in_sem, a_send, a_recv, b_send, b_recv, l_send, r_send, y_sem, l_sem, n_sem, r_sem, c_sem,
):
    yh_n, z_n, yl_n, x_n = dims
    ns, nr = yh_n * z_n, yl_n * x_n * 2
    half_n, zh_n = ns // 2, z_n // 2
    rows = x_ref.shape[0]
    sl = rows // ns
    block = rows // 2
    me_s, me_r = lax.axis_index("seq"), lax.axis_index("res")
    yh, z = lax.div(me_s, z_n), lax.rem(me_s, z_n)
    core, x, yl = lax.rem(me_r, 2), lax.rem(lax.div(me_r, 2), x_n), lax.div(me_r, 2 * x_n)
    zh = lax.div(z, 2)
    slot = lax.rem(z, 2) * half_n + yh * zh_n + zh

    def seq_id(b, dz):
        return lax.rem(yh + b, yh_n) * z_n + lax.rem(z + dz + z_n, z_n)

    def left_at(b, dz):
        return lax.rem(z + dz + z_n, z_n) * yh_n + lax.rem(yh + b, yh_n)

    def res_of(b, dx, core_):
        return (lax.rem(yl + b, yl_n) * x_n + lax.rem(x + dx + x_n, x_n)) * 2 + core_

    loads = [
        pltpu.make_async_copy(src, dst, in_sem.at[i])
        for i, (src, dst) in enumerate((
            (tok_h, tok_ref), (table_h, table_ref), (x_h, x_ref), (mask_h, mask_ref), (wq_h, wq_ref), (wk_h, wk_ref), (wv_h, wv_ref), (wg_h, wg_ref), (wo_h, wo_ref),
            (w1_h, wt.at[pl.ds(768, 32)]), (w2_h, wt.at[pl.ds(800, 32)]), (pw_h, pw_ref),
        ))
    ]
    for load in loads[:3]:
        load.start()

    barrier = pltpu.get_barrier_semaphore()

    def greet(off, carry):
        pl.semaphore_signal(barrier, inc=1, device_id=(lax.rem(me_s + off, ns), me_r), device_id_type=MESH)
        return carry

    lax.fori_loop(1, ns, greet, 0)
    for peer in (res_of(0, 0, 1 - core), res_of(1, 0, core), res_of(0, 1, core), res_of(0, -1, core)):
        pl.semaphore_signal(barrier, inc=1, device_id=(me_s, peer), device_id_type=MESH)
    for load in loads[3:]:
        load.start()

    n_rows = iota((rows, rows), 0)
    n_cols = iota((rows, rows), 1)
    sl_bits, ns_bits = sl.bit_length() - 1, ns.bit_length() - 1
    pick = one_hot(n_cols == (n_rows & (sl - 1)) * ns + (n_rows >> sl_bits))
    loads[0].wait()
    loads[1].wait()
    n_seq = iota((rows, sl), 0) & (sl - 1)
    token_rows = dot(one_hot(iota((rows, sl), 1) == n_seq), tok_ref[...].astype(F32).astype(BF16))
    own = (iota((rows, ns), 0) >> sl_bits) == iota((rows, ns), 1)
    token = jnp.sum(jnp.where(own, token_rows, 0.0), axis=1, keepdims=True)
    kinds = table_ref.shape[0]
    table_s[...] = jnp.zeros_like(table_s)
    table_s[0:kinds, :] = table_ref[...].astype(F32)
    classes = table_s.shape[0]
    token_hot = one_hot(iota((rows, classes), 1).astype(F32) == token)
    embedded = dot(token_hot, table_s[...].astype(BF16))
    loads[2].wait()
    msa = (dot(pick, x_ref[...]) + embedded).astype(BF16)
    snd[...] = msa.reshape(snd.shape)
    col[pl.ds(slot, 1)] = snd[pl.ds(me_s, 1)]

    pl.semaphore_wait(barrier, ns - 1 + 4)

    def send_out(t, carry):
        off = lax.rem(t * 11, ns)
        to = lax.rem(yh + lax.div(off, z_n), yh_n) * z_n + lax.rem(z + lax.rem(off, z_n), z_n)
        pltpu.make_async_remote_copy(
            src_ref=snd.at[to], dst_ref=col.at[slot], send_sem=a_send, recv_sem=a_recv,
            device_id=(to, me_r), device_id_type=MESH,
        ).start()
        return carry

    lax.fori_loop(1, ns, send_out, 0)

    for load in loads[3:]:
        load.wait()
    wt[0:256, :] = turned(wq_ref[...])
    wt[256:512, :] = turned(wv_ref[...])
    wt[512:768, :] = turned(wg_ref[...])
    live_all = jnp.where(iota((16, rows), 1) == 0, 1, mask_ref[...]).astype(F32)
    count = jnp.sum(live_all[0:1], axis=1, keepdims=True) + 0.001
    place = n_cols >> sl_bits
    spot = place & (half_n - 1)
    zh_bits = zh_n.bit_length() - 1
    device = (spot >> zh_bits) * z_n + (spot & (zh_n - 1)) * 2 + jnp.where(place >= half_n, 1, 0)
    order = one_hot(n_rows == device * sl + (n_cols & (sl - 1)))
    live = dot(live_all.astype(BF16), order)[0:1]
    live_col = jnp.sum(jnp.where(n_rows == n_cols, live, 0.0), axis=1, keepdims=True)
    bias[...] = jnp.broadcast_to((live_col - 1.0) * 1e9, bias.shape)
    wide = nr * 32
    turn = iota((256, 256), 0)
    perm[...] = one_hot(iota((256, 256), 1) == (turn & 7) * 32 + (turn >> 3))
    pw_s[...] = pw_ref[...].astype(F32)
    w4[...] = jnp.zeros_like(w4)

    def spread(e, carry):
        part = pw_s[pl.ds(e, 32, stride=32), :].astype(BF16)
        for i in range(4):
            w4[pl.ds(pl.multiple_of(e * 128 + i * 32, 32), 32), i * 128 : (i + 1) * 128] = part
        return carry

    lax.fori_loop(0, 32, spread, 0)

    pltpu.make_async_copy(snd.at[pl.ds(0, ns - 1)], col.at[pl.ds(0, ns - 1)], a_recv).wait()

    normed = standardize(col[...].reshape(rows, 256).astype(F32)).astype(BF16)
    k_s[...] = dot(normed, wk_ref[...]).astype(BF16)
    q_t[...] = dot_nt(wt[0:256, :], normed).astype(BF16).astype(F32)
    v_t[...] = dot_nt(wt[256:512, :], normed).astype(BF16)
    g_t[...] = jax.nn.sigmoid(dot_nt(wt[512:768, :], normed).astype(BF16).astype(F32))
    factor = SUB**-0.5 * math.log2(math.e)

    def scores_of(h, part):
        at = pl.multiple_of(lax.div(h, 4) * 128, 128)
        query = jnp.where((iota((128, block), 0) >> 5) == lax.rem(h, 4), q_t[pl.ds(at, 128), part], 0.0).astype(BF16)
        return dot(k_s[:, pl.ds(at, 128)], query) + bias[...]

    def weigh(h, part, scores):
        here = pl.multiple_of(h * SUB, SUB)
        top = jnp.max(scores, axis=0, keepdims=True)
        weights = jnp.exp2((scores - top) * factor)
        total = jnp.sum(weights, axis=0, keepdims=True)
        ctx[pl.ds(here, SUB), part] = dot(v_t[pl.ds(here, SUB), :], weights.astype(BF16)) / total

    def attend(b):
        part = slice(b * block, (b + 1) * block)

        def heads(h, carry):
            ahead = scores_of(h * 4, part)
            for j in range(4):
                scores, ahead = ahead, scores_of(h * 4 + j + 1, part) if j < 3 else None
                weigh(h * 4 + j, part, scores)
            return carry

        lax.fori_loop(0, HEADS // 4, heads, 0)
        gated = (g_t[:, part] * ctx[:, part]).T.astype(BF16)
        column = col[b * half_n : (b + 1) * half_n].reshape(block, 256).astype(F32)
        revised = (column + dot(gated, wo_ref[...])).astype(BF16)
        snd2[b * half_n : (b + 1) * half_n] = revised.reshape(half_n, sl, 256)
        again = standardize(revised.astype(F32)).astype(BF16)
        fac[:, part] = (dot_nt(wt[768:832, :], again) * live[:, part]).astype(BF16)

    def send_back(b, first, last):
        def one(t, carry):
            off = lax.rem(t * 5, half_n)
            to_y = lax.rem(yh + lax.div(off, zh_n), yh_n)
            to_z = lax.rem(zh + lax.rem(off, zh_n), zh_n)
            to = to_y * z_n + to_z * 2 + b

            @pl.when(to != me_s)
            def _():
                pltpu.make_async_remote_copy(
                    src_ref=snd2.at[b * half_n + to_y * zh_n + to_z], dst_ref=back.at[me_s],
                    send_sem=b_send, recv_sem=b_recv, device_id=(to, me_r), device_id_type=MESH,
                ).start()

            return carry

        lax.fori_loop(first, last, one, 0)

    def part_of(buf, at, half):
        return buf.at[at] if half is None else buf.at[at, pl.ds(16 * half, 16)]

    def push(buf, at, dev, send, recv, half=None):
        ref = part_of(buf, at, half)
        pltpu.make_async_remote_copy(
            src_ref=ref, dst_ref=ref, send_sem=send, recv_sem=recv, device_id=dev, device_id_type=MESH
        ).start()

    def arrived(buf, at, recv, half=None):
        ref = part_of(buf, at, half)
        pltpu.make_async_copy(ref, ref, recv).wait()

    def ring(buf, n, index, device, send, sems):
        far = n // 2

        def give(b, way, k):
            step = 1 - 2 * way
            half = way if k + 1 == far else None
            push(buf, index(b, -step * k), device(step), send, sems.at[(b * 2 + way) * far + k], half)

        def take(b, way, k):
            step = 1 - 2 * way
            half = way if k == far else None
            arrived(buf, index(b, -step * k), sems.at[(b * 2 + way) * far + k - 1], half)

        return far, give, take

    l_far, l_give, l_take = ring(lt, z_n, left_at, lambda s: (seq_id(0, s), me_r), l_send, l_sem)
    r_far, r_give, r_take = ring(
        rt, x_n, lambda b, d: res_of(b, d, core), lambda s: (me_s, res_of(0, s, core)), r_send, r_sem
    )
    mate = (me_s, res_of(0, 0, 1 - core))

    def hand_over(b, dx):
        push(rt, res_of(b, dx, core), mate, r_send, c_sem.at[b * x_n + dx % x_n])

    def r_step(k):
        for b in range(2):
            for way in range(2):
                r_take(b, way, k)
                if k < r_far:
                    r_give(b, way, k)
                    hand_over(b, k * (2 * way - 1))
            if k == r_far:
                hand_over(b, k)

    def l_step(k):
        for b in range(yh_n):
            for way in range(2):
                l_take(b, way, k)
                if k < l_far:
                    l_give(b, way, k)

    attend(0)
    send_back(0, 0, half_n)
    attend(1)
    lt[pl.ds(left_at(0, 0), 1)] = fac[0:32, :].reshape(1, 32, rows)
    rt[pl.ds(me_r, 1)] = fac[32:64, :].reshape(1, 32, rows)
    back[pl.ds(me_s, 1)] = snd2[pl.ds(slot, 1)]

    def start_row():
        push(rt, me_r, (me_s, res_of(1, 0, core)), r_send, n_sem)

    def start_rings():
        for way in range(2):
            l_give(0, way, 0)
            r_give(0, way, 0)

    def start_columns():
        for b in range(1, yh_n):
            push(lt, left_at(0, 0), (seq_id(b, 0), me_r), l_send, y_sem.at[yh_n - b - 1])

    def next_row():
        arrived(rt, res_of(1, 0, core), n_sem)
        for way in range(2):
            r_give(1, way, 0)
        hand_over(1, 0)

    def next_column(b):
        arrived(lt, left_at(b, 0), y_sem.at[b - 1])
        for way in range(2):
            l_give(b, way, 0)

    def r_step(b, k):
        if 1 <= k <= r_far:
            for way in range(2):
                r_take(b, way, k)
                if k < r_far:
                    r_give(b, way, k)
                    hand_over(b, k * (2 * way - 1))
            if k == r_far:
                hand_over(b, k)

    def l_step(b, k):
        if 1 <= k <= l_far:
            for way in range(2):
                l_take(b, way, k)
                if k < l_far:
                    l_give(b, way, k)

    def right_rows():
        for b in range(2):
            for dx in range(x_n):
                arrived(rt, res_of(b, dx, 1 - core), c_sem.at[b * x_n + dx])
        for n in range(nr // 8):
            eight = rt[n * 8 : (n + 1) * 8].reshape(256, rows)
            rp[n * 256 : (n + 1) * 256, :] = dot(perm[...], eight).astype(BF16)

    groups = []

    def outer_part(*distances):
        lefts = []
        for dz in distances:
            group = lax.rem(z + dz + z_n, z_n)
            groups.append(group)
            lefts.append(lt[pl.ds(group * yh_n, yh_n)].reshape(yh_n * 32, rows))
        product = dot_nt(rp[...], jnp.concatenate(lefts, axis=0))
        for j in range(len(distances)):
            to = (len(groups) - len(distances) + j) * nr
            for e in range(32):
                lane = slice(j * 128, (j + 1) * 128)
                eights = [product[n * 256 + e * 8 : n * 256 + (e + 1) * 8, lane] for n in range(nr // 8)]
                lhs[to : to + nr, e * 128 : (e + 1) * 128] = jnp.concatenate(eights, axis=0).astype(BF16)

    sent = 0
    for word in SCHEDULE:
        kind, args = word[0], [int(c) for c in word[1:]]
        if kind == "r":
            start_row()
            hand_over(0, 0)
        elif kind == "s":
            start_rings()
        elif kind == "c":
            start_columns()
        elif kind == "N":
            next_row()
        elif kind == "Y":
            next_column(*args)
        elif kind == "R":
            r_step(*args)
        elif kind == "L":
            l_step(*args)
        elif kind == "P":
            right_rows()
        elif kind == "B":
            more = min(args[0], half_n - sent)
            send_back(1, sent, sent + more)
            sent += more
        elif kind == "O":
            if args[0] < l_far:
                outer_part(-args[0], args[0])
            elif args[0] == l_far:
                outer_part(0, l_far)

    pair = dot(lhs[...], w4[...]) / count
    for n, group in enumerate(groups):
        for i in range(4):
            pair_ref[i * z_n + group] = pair[n * nr : (n + 1) * nr, i * 128 : (i + 1) * 128]

    pltpu.make_async_copy(snd2.at[pl.ds(0, ns - 1)], back.at[pl.ds(0, ns - 1)], b_recv).wait()
    unpick = one_hot(n_cols == (n_rows & (ns - 1)) * sl + (n_rows >> ns_bits))
    rev_ref[...] = dot(unpick, back[...].reshape(rows, 256)).astype(BF16)

    pltpu.make_async_copy(snd.at[pl.ds(0, ns - 1)], snd.at[pl.ds(0, ns - 1)], a_send).wait()
    pltpu.make_async_copy(snd2.at[pl.ds(0, ns - 1)], snd2.at[pl.ds(0, ns - 1)], b_send).wait()
    pltpu.make_async_copy(lt.at[pl.ds(0, ns - 1)], lt.at[pl.ds(0, ns - 1)], l_send).wait()
    pltpu.make_async_copy(rt.at[pl.ds(0, nr - 1)], rt.at[pl.ds(0, nr - 1)], r_send).wait()


def per_device(dims, features, tokens, mask, table, wq, wk, wv, wg, wo, w1, w2, pw):
    yh_n, z_n, yl_n, x_n = dims
    ns, nr = yh_n * z_n, yl_n * x_n * 2
    sl, res_local, width = features.shape
    rows = sl * res_local
    vmem, hbm = pl.BlockSpec(memory_space=pltpu.VMEM), pl.BlockSpec(memory_space=pltpu.HBM)
    dma = pltpu.SemaphoreType.DMA
    revised, pair = pl.pallas_call(
        functools.partial(kernel, dims),
        out_shape=(
            jax.ShapeDtypeStruct((rows, width), BF16),
            jax.ShapeDtypeStruct((ns, nr, pw.shape[1]), F32),
        ),
        in_specs=[hbm] * 12,
        out_specs=(vmem, vmem),
        scratch_shapes=[
            pltpu.VMEM((rows, width), BF16),
            pltpu.VMEM(tokens.shape, I32),
            pltpu.VMEM((1, rows), I32),
            pltpu.VMEM(table.shape, BF16),
            *[pltpu.VMEM((width, width), BF16)] * 5,
            pltpu.VMEM(pw.shape, BF16),
            *[pltpu.VMEM((ns, sl, width), BF16)] * 4,
            pltpu.VMEM((ns, 32, rows), BF16),
            pltpu.VMEM((nr, 32, rows), BF16),
            pltpu.VMEM((256, rows), F32),
            pltpu.VMEM((rows, 256), BF16),
            pltpu.VMEM((256, rows), BF16),
            pltpu.VMEM((256, rows), F32),
            pltpu.VMEM((256, rows), F32),
            pltpu.VMEM((rows, rows // 2), F32),
            pltpu.VMEM((32, width), F32),
            pltpu.VMEM(pw.shape, F32),
            pltpu.VMEM((32 * 128, 512), BF16),
            pltpu.VMEM((832, 256), BF16),
            pltpu.VMEM((256, 256), BF16),
            pltpu.VMEM((nr * 32, rows), BF16),
            pltpu.VMEM((64, rows), BF16),
            pltpu.VMEM((z_n * nr, 32 * 128), BF16),
            dma((12,)),
            dma, dma, dma, dma, dma, dma,
            dma((yh_n - 1,)),
            dma((yh_n * z_n,)),
            dma,
            dma((yl_n * x_n,)),
            dma((yl_n * x_n,)),
        ],
        compiler_params=pltpu.CompilerParams(
            collective_id=0, has_side_effects=True, vmem_limit_bytes=VMEM_BYTES
        ),
    )(
        *[
            pltpu.with_memory_space_constraint(a, pltpu.HBM)
            for a in (
                features.reshape(rows, width), tokens, mask.reshape(1, -1), table,
                wq, wk, wv, wg, wo, w1.T, w2.T, pw,
            )
        ]
    )
    return revised.reshape(features.shape), pair.reshape(ns, 1, nr, pw.shape[1])


def solution(mesh, dims=DIMS):
    return jax.shard_map(
        functools.partial(per_device, dims),
        mesh=mesh,
        in_specs=(P("seq", "res", None), P("seq", "res")) + (P(),) * 10,
        out_specs=(P("seq", "res", None), P("res", "seq", None, None)),
        check_vma=False,
    )
```
